256 devices in a mesh: wave: 32 (over z, x), lev: 8 (over y, core).
Axes of the slice: x: 4, y: 4, z: 8, core: 2. Of those that a mesh axis runs over, the one named last changes fastest.
Arguments:
- legendre_values: bfloat16 [1280, 512, 1280], P(('wave', 'lev')), may hold values from -0.15625 to 0.15625
- spectra: bfloat16 [1280, 1280, 128], P(('wave', 'lev')), may hold values from -0.16699219 to 0.16699219
- wave_table: int32 [1280], replicated, may hold values from 0 to 1279, each once
- row_longitudes: int32 [512], P(('wave', 'lev')), may hold values from 20 to 5136, as said below
Outputs:
- grid_fields: float32 [512, 64, 5376], P(('wave', 'lev'))
The draws below stay inside these ranges and needn't reach their ends.
Inputs may be any that keep to these rules, and one draw needn't show every extreme that they name: `wave_table`: every wavenumber appears in exactly one slot. `row_longitudes`: each count is 20 plus a multiple of 4; some row of every draw has 5136.
All inputs are finite; a program needn't handle non-finite values.
Results may differ from the reference program's by a relative error of at most 0.0003.
Values sent between devices are 32-bit elements; how exact they have to be, the bound alone decides.
A program may use at most 128 MiB of HBM per device.

```python
import jax
import jax.numpy as jnp
from jax import lax

M = 1280
CH = 128
NLAT = 512
NLON = 5376


def draw_row_longitudes(key, part):
    first_key, second_key = jax.random.split(jax.random.fold_in(key, 17))
    steps_drawn = jax.random.randint(first_key, (NLAT,), 0, M)
    chosen_row = jax.random.randint(second_key, (), 0, NLAT)
    steps_drawn = jnp.where(jnp.arange(NLAT) == chosen_row, M - 1, steps_drawn)
    return (20 + 4 * steps_drawn).astype(jnp.int32)


def levels(rng, extent, cuts, smallest, largest):
    def one(position, shards_of):
        draws = jax.random.uniform(jax.random.fold_in(jax.random.fold_in(rng, 6), position), (shards_of,), jnp.float32, smallest / len(cuts), largest / len(cuts))
        return jnp.repeat(jnp.exp(draws), extent[position] // shards_of).reshape((-1,) + (1,) * (len(extent) - position - 1))

    gain = one(*cuts[0])
    for cut in cuts[1:]:
        gain = gain * one(*cut)
    return gain


def normal_values(stream_key, dims, spread, reach, shards=(), kind=jnp.bfloat16):
    loudness = levels(stream_key, dims, shards, -0.22, 0.18) if shards else 1.0
    entries = jax.random.normal(stream_key, dims, jnp.float32) * spread * loudness
    return jnp.minimum(jnp.maximum(entries, -reach), reach).astype(kind)


def setup_inputs(seed: int = 0) -> dict:
    seeds = jax.random.split(jax.random.key(seed), 5)
    return {
        "legendre_values": normal_values(seeds[0], (M, NLAT, M), M ** -0.5, 0.15625, ((0, 256),)),
        "spectra": normal_values(seeds[1], (M, M, CH), (1.0 / M ** 0.5), 0.16699219, ((0, 256),)),
        "wave_table": jax.random.permutation(seeds[2], M).astype(jnp.int32),
        "row_longitudes": draw_row_longitudes(jax.random.fold_in(seeds[4], 71), 0),
    }


def reference(legendre_values, spectra, wave_table, row_longitudes):
    degrees = jnp.arange(M, dtype=jnp.int32)

    def legendre_one(items):
        values, coefficients, wavenumber = items
        kept = jnp.where((degrees >= wavenumber)[:, None], coefficients, jnp.zeros_like(coefficients))
        return jnp.dot(values, kept, preferred_element_type=jnp.float32)

    fourier = lax.map(legendre_one, (legendre_values, spectra, wave_table))
    columns = jnp.arange(NLON, dtype=jnp.int32)
    base_weight = jnp.where(wave_table == 0, jnp.float32(1.0), jnp.float32(2.0))

    def row_one(items):
        coefficients, longitudes = items
        pairs = coefficients.astype(jnp.float32).reshape(M, CH // 2, 2)
        weight = jnp.where(wave_table <= (longitudes - 1) // 2, base_weight, jnp.float32(0.0))
        real_part = pairs[:, :, 0] * weight[:, None]
        imag_part = pairs[:, :, 1] * weight[:, None]
        phase = (wave_table[:, None] * columns[None, :]) % longitudes
        angle = phase.astype(jnp.float32) * (jnp.float32(2.0 * jnp.pi) / longitudes.astype(jnp.float32))
        values = jnp.dot(real_part.T, jnp.cos(angle), precision=lax.Precision.HIGHEST)
        values = values - jnp.dot(imag_part.T, jnp.sin(angle), precision=lax.Precision.HIGHEST)
        return jnp.where(columns[None, :] < longitudes, values, jnp.float32(0.0))

    return lax.map(row_one, (jnp.swapaxes(fourier, 0, 1), row_longitudes))
```

```python
import functools

import jax
import jax.numpy as jnp
from jax import lax
from jax.experimental import pallas as pl
from jax.experimental.pallas import tpu as pltpu
from jax.sharding import PartitionSpec as P

MESH = pl.DeviceIdType.MESH

SLOTS = 5
DEGREES = 1280
ROWS = 512
CHANNELS = 128
FIELDS = 64
LOCAL_ROWS = 2
DEVICES = 256
NLON = 5376
HALF = 256
SPAN = 2 * HALF
BLOCKS = 11
STACKED = BLOCKS * FIELDS

COS_TERMS = (
    0.9999999996168156,
    -19.73920863354667,
    64.93938183835107,
    -85.4564814603686,
    60.24009011425828,
    -26.392650988301078,
    7.765225095262238,
    -1.4134373617596543,
)
SIN_TERMS = (
    6.283185293777215,
    -41.341697721207424,
    81.605000209223,
    -76.70070302960839,
    42.00769493017941,
    -14.834123486306066,
    3.1498534224128543,
)


def horner(terms, square):
    total = jnp.full_like(square, terms[-1])
    for term in terms[-2::-1]:
        total = total * square + jnp.float32(term)
    return total


def cos_sin_of_turns(product, period, inverse):
    whole = jnp.round(product * inverse)
    turn = (product - whole * period) * inverse
    square = turn * turn
    return horner(COS_TERMS, square), turn * horner(SIN_TERMS, square)


def split(values):
    high = values.astype(jnp.bfloat16)
    low = (values - high.astype(jnp.float32)).astype(jnp.bfloat16)
    return high, low


def legendre_sums(wave_table, legendre_values, spectra):
    me = lax.axis_index("wave") * lax.axis_size("lev") + lax.axis_index("lev")
    wavenumbers = lax.dynamic_slice_in_dim(wave_table, me * SLOTS, SLOTS)
    degrees = jnp.arange(DEGREES, dtype=jnp.int32)
    allowed = degrees[None, :] >= wavenumbers[:, None]
    kept = jnp.where(allowed[:, :, None], spectra, jnp.zeros_like(spectra))
    return jnp.einsum("srn,snc->src", legendre_values, kept, preferred_element_type=jnp.float32)


def exchange(wave_table, legendre_values, spectra):
    fourier = legendre_sums(wave_table, legendre_values, spectra)
    moved = lax.all_to_all(fourier, ("wave", "lev"), split_axis=1, concat_axis=1, tiled=True)
    return jnp.swapaxes(moved.reshape(SLOTS, DEVICES, LOCAL_ROWS, CHANNELS), 1, 2)


def rows_kernel(longitudes_ref, waves_ref, arrived_ref, out_ref, turned, cos_sum, sin_sum):
    longitudes = longitudes_ref[pl.program_id(0)]
    period = (2 * longitudes).astype(jnp.float32)
    period_row = jnp.full((8, 128), period, jnp.float32)
    inverse = (jnp.float32(1.0) / period_row)[:1, :1]
    largest = lax.div(longitudes - 1, 2).astype(jnp.float32)
    odd = (2 * lax.broadcasted_iota(jnp.int32, (HALF, HALF), 1) + 1).astype(jnp.float32)
    centre = (
        2 * SPAN * lax.broadcasted_iota(jnp.int32, (16, HALF), 0) + (SPAN - 1)
    ).astype(jnp.float32)
    cos_sum[...] = jnp.zeros_like(cos_sum)
    sin_sum[...] = jnp.zeros_like(sin_sum)

    def slot_step(slot, carry):
        wave_row = waves_ref[pl.ds(slot, 1), :].astype(jnp.float32)
        wave_column = jnp.broadcast_to(wave_row, (HALF, HALF)).T
        table_cos, table_sin = cos_sin_of_turns(wave_column * odd, period, inverse)
        cos_high, cos_low = split(table_cos)
        sin_high, sin_low = split(table_sin)
        cos_table = jnp.concatenate([cos_high, cos_high, cos_low], axis=0)
        sin_table = jnp.concatenate([sin_high, sin_high, sin_low], axis=0)
        block_cos, block_sin = cos_sin_of_turns(wave_row * centre, period, inverse)
        weight = jnp.where(
            wave_row > largest,
            jnp.float32(0.0),
            jnp.where(wave_row == 0, jnp.float32(1.0), jnp.float32(2.0)),
        )
        for half in range(2):
            turned[half] = arrived_ref[slot, 0, pl.ds(half * 128, 128), :].T
        real, imag = (
            jnp.concatenate(
                [turned[half, pl.ds(part, FIELDS, stride=2), :] for half in range(2)], axis=1
            )
            * weight
            for part in range(2)
        )
        real_parts = []
        imag_parts = []
        for k in range(BLOCKS):
            c = block_cos[k : k + 1, :]
            s = block_sin[k : k + 1, :]
            high, low = split(real * c - imag * s)
            real_parts.append(jnp.concatenate([high, low, high], axis=1))
            high, low = split(real * s + imag * c)
            imag_parts.append(jnp.concatenate([high, low, high], axis=1))
        real_side = jnp.concatenate(real_parts, axis=0)
        imag_side = jnp.concatenate(imag_parts, axis=0)
        cos_sum[...] += jnp.dot(real_side, cos_table, preferred_element_type=jnp.float32)
        sin_sum[...] += jnp.dot(imag_side, sin_table, preferred_element_type=jnp.float32)
        return carry

    lax.fori_loop(0, SLOTS, slot_step, 0)
    backwards = 127 - lax.broadcasted_iota(jnp.int32, (FIELDS, 128), 1)
    column = lax.broadcasted_iota(jnp.int32, (FIELDS, 128), 1)
    for k in range(BLOCKS):
        rows = pl.ds(k * FIELDS, FIELDS)
        for part in range(2):
            lanes = pl.ds(part * 128, 128)
            c = cos_sum[rows, lanes]
            s = sin_sum[rows, lanes]
            first = k * SPAN + 128 * (1 - part)
            values = jnp.take_along_axis(c + s, backwards, axis=1)
            out_ref[0, :, pl.ds(first, 128)] = jnp.where(
                column + first < longitudes, values, jnp.float32(0.0)
            )
            first = k * SPAN + HALF + 128 * part
            if first < NLON:
                out_ref[0, :, pl.ds(first, 128)] = jnp.where(
                    column + first < longitudes, c - s, jnp.float32(0.0)
                )


def rows_transform(row_longitudes, waves, arrived, interpret=False):
    return pl.pallas_call(
        rows_kernel,
        out_shape=jax.ShapeDtypeStruct((LOCAL_ROWS, FIELDS, NLON), jnp.float32),
        grid=(LOCAL_ROWS,),
        in_specs=[
            pl.BlockSpec(memory_space=pltpu.SMEM),
            pl.BlockSpec(memory_space=pltpu.VMEM),
            pl.BlockSpec((SLOTS, 1, DEVICES, CHANNELS), lambda r: (0, r, 0, 0)),
        ],
        out_specs=pl.BlockSpec((1, FIELDS, NLON), lambda r: (r, 0, 0)),
        scratch_shapes=[
            pltpu.VMEM((2, CHANNELS, 128), jnp.float32),
            pltpu.VMEM((STACKED, HALF), jnp.float32),
            pltpu.VMEM((STACKED, HALF), jnp.float32),
        ],
        compiler_params=pltpu.CompilerParams(vmem_limit_bytes=40 << 20),
        interpret=interpret,
    )(row_longitudes, waves, arrived)


def per_device(legendre_values, spectra, wave_table, row_longitudes):
    waves = wave_table.reshape(DEVICES, SLOTS).T
    arrived = exchange(wave_table, legendre_values, spectra)
    return rows_transform(row_longitudes, waves, arrived)


def solution(mesh):
    in_specs = (
        P(("wave", "lev"), None, None),
        P(("wave", "lev"), None, None),
        P(),
        P(("wave", "lev")),
    )
    out_specs = P(("wave", "lev"), None, None)
    return jax.shard_map(
        per_device, mesh=mesh, in_specs=in_specs, out_specs=out_specs, check_vma=False
    )
```

```python
import functools

import jax
import jax.numpy as jnp
from jax import lax
from jax.experimental import pallas as pl
from jax.experimental.pallas import tpu as pltpu
from jax.sharding import PartitionSpec as P

MESH = pl.DeviceIdType.MESH

SLOTS = 5
DEGREES = 1280
ROWS = 512
CHANNELS = 128
FIELDS = 64
LOCAL_ROWS = 2
PLANES = 8
PER_PLANE = 4
WAVES = PLANES * PER_PLANE
LEVS = 8
DEVICES = WAVES * LEVS
NLON = 5376
HALF = 256
SPAN = 2 * HALF
BLOCKS = 11
STACKED = BLOCKS * FIELDS

COS_TERMS = (
    0.9999999996168156,
    -19.73920863354667,
    64.93938183835107,
    -85.4564814603686,
    60.24009011425828,
    -26.392650988301078,
    7.765225095262238,
    -1.4134373617596543,
)
SIN_TERMS = (
    6.283185293777215,
    -41.341697721207424,
    81.605000209223,
    -76.70070302960839,
    42.00769493017941,
    -14.834123486306066,
    3.1498534224128543,
)


def horner(terms, square):
    total = jnp.full_like(square, terms[-1])
    for term in terms[-2::-1]:
        total = total * square + jnp.float32(term)
    return total


def cos_sin_of_turns(product, period, inverse):
    whole = jnp.round(product * inverse)
    turn = (product - whole * period) * inverse
    square = turn * turn
    return horner(COS_TERMS, square), turn * horner(SIN_TERMS, square)


def split(values):
    high = values.astype(jnp.bfloat16)
    low = (values - high.astype(jnp.float32)).astype(jnp.bfloat16)
    return high, low


def exchange_kernel(
    table_ref, legendre_ref, spectra_ref, out_ref,
    legendre, spectra, fourier, by_lev, by_x, by_z,
    load_sem, send_sem, lev_sem, x_sem, z_sem, own_sem, out_sem,
):
    wave = lax.axis_index("wave")
    lev = lax.axis_index("lev")
    z, x = lax.div(wave, PER_PLANE), lax.rem(wave, PER_PLANE)
    me = wave * LEVS + lev
    lev_peers = [lax.rem(lev + k, LEVS) for k in range(1, LEVS)]
    x_peers = [lax.rem(x + k, PER_PLANE) for k in range(1, PER_PLANE)]
    z_peers = [lax.rem(z + k, PLANES) for k in (4, 3, 5, 2, 6, 1, 7)]

    def load(slot):
        return (
            pltpu.make_async_copy(spectra_ref.at[slot], spectra.at[slot], load_sem.at[0, slot]),
            pltpu.make_async_copy(legendre_ref.at[slot], legendre.at[slot], load_sem.at[1, slot]),
        )

    for slot in range(SLOTS):
        for copy in load(slot):
            copy.start()

    barrier = pltpu.get_barrier_semaphore()
    for peer in z_peers:
        pl.semaphore_signal(
            barrier, inc=1, device_id=(peer * PER_PLANE + x, lev), device_id_type=MESH
        )
    for peer in x_peers:
        pl.semaphore_signal(
            barrier, inc=1, device_id=(z * PER_PLANE + peer, lev), device_id_type=MESH
        )
    for peer in lev_peers:
        pl.semaphore_signal(barrier, inc=1, device_id=(wave, peer), device_id_type=MESH)

    degree = lax.broadcasted_iota(jnp.int32, (DEGREES, CHANNELS), 0)

    def legendre_step(slot):
        for copy in load(slot):
            copy.wait()
        wavenumber = table_ref[me * SLOTS + slot]
        values = spectra[slot].astype(jnp.float32)
        kept = jnp.where(degree >= wavenumber, values, jnp.float32(0.0)).astype(jnp.bfloat16)
        sums = jnp.dot(legendre[slot], kept, preferred_element_type=jnp.float32)
        fourier[slot] = sums.reshape(WAVES, LEVS * LOCAL_ROWS, CHANNELS)

    def move(source, target, peers, own, where, stage, slot, recv):
        for peer in peers:
            pltpu.make_async_remote_copy(
                src_ref=source(peer),
                dst_ref=target,
                send_sem=send_sem.at[stage],
                recv_sem=recv.at[slot],
                device_id=where(peer),
                device_id_type=MESH,
            ).start()
        pltpu.make_async_copy(source(own), target, own_sem.at[stage, slot]).start()

    def move_lev(slot):
        move(
            lambda peer: fourier.at[slot, :, pl.ds(peer * LOCAL_ROWS, LOCAL_ROWS), :],
            by_lev.at[slot, :, :, lev, :],
            lev_peers, lev, lambda peer: (wave, peer), 0, slot, lev_sem,
        )

    def move_x(slot):
        move(
            lambda peer: by_lev.at[slot].reshape(
                PLANES, PER_PLANE, LOCAL_ROWS, LEVS, CHANNELS
            ).at[:, peer],
            by_x.at[slot, :, :, x],
            x_peers, x, lambda peer: (z * PER_PLANE + peer, lev), 1, slot, x_sem,
        )

    def move_z(slot):
        move(
            lambda peer: by_x.at[slot, peer],
            by_z.at[slot, :, z],
            z_peers, z, lambda peer: (peer * PER_PLANE + x, lev), 2, slot, z_sem,
        )

    def arrived(source, target, region, stage, slot, recv):
        pltpu.make_async_copy(region, region, recv.at[slot]).wait()
        pltpu.make_async_copy(source, target, own_sem.at[stage, slot]).wait()

    def lev_arrived(slot):
        arrived(
            fourier.at[slot, :, pl.ds(0, LOCAL_ROWS), :], by_lev.at[slot, :, :, 0, :],
            by_lev.at[slot, pl.ds(0, 28)], 0, slot, lev_sem,
        )

    def x_arrived(slot):
        arrived(
            by_x.at[slot, :, :, 0], by_x.at[slot, :, :, 0],
            by_x.at[slot, pl.ds(0, 6)], 1, slot, x_sem,
        )

    def z_arrived(slot):
        arrived(
            by_x.at[slot, 0], by_z.at[slot, :, 0],
            by_z.at[slot, :, pl.ds(0, 7)], 2, slot, z_sem,
        )

    legendre_step(0)
    pl.semaphore_wait(barrier, LEVS + PER_PLANE + PLANES - 3)
    move_lev(0)
    for slot in range(1, SLOTS):
        legendre_step(slot)
        move_lev(slot)
    for turn in range(SLOTS + 1):
        if turn < SLOTS:
            lev_arrived(turn)
            move_x(turn)
        if turn >= 1:
            x_arrived(turn - 1)
            move_z(turn - 1)
    for slot in range(SLOTS):
        z_arrived(slot)
        pltpu.make_async_copy(by_z.at[slot], out_ref.at[slot], out_sem).start()
    pltpu.make_async_copy(by_lev.at[:, pl.ds(0, 28)], by_lev.at[:, pl.ds(0, 28)], send_sem.at[0]).wait()
    pltpu.make_async_copy(by_x.at[:, pl.ds(0, 6)], by_x.at[:, pl.ds(0, 6)], send_sem.at[1]).wait()
    pltpu.make_async_copy(by_x.at[:, pl.ds(0, 7)], by_x.at[:, pl.ds(0, 7)], send_sem.at[2]).wait()
    pltpu.make_async_copy(by_z, out_ref, out_sem).wait()


def exchange(wave_table, legendre_values, spectra):
    any_space = pl.BlockSpec(memory_space=pl.ANY)
    final = (SLOTS, LOCAL_ROWS, PLANES, PER_PLANE, LEVS, CHANNELS)
    return pl.pallas_call(
        exchange_kernel,
        out_shape=jax.ShapeDtypeStruct(final, jnp.float32),
        in_specs=[pl.BlockSpec(memory_space=pltpu.SMEM), any_space, any_space],
        out_specs=any_space,
        scratch_shapes=[
            pltpu.VMEM((SLOTS, ROWS, DEGREES), jnp.bfloat16),
            pltpu.VMEM((SLOTS, DEGREES, CHANNELS), jnp.bfloat16),
            pltpu.VMEM((SLOTS, WAVES, LEVS * LOCAL_ROWS, CHANNELS), jnp.float32),
            pltpu.VMEM((SLOTS, WAVES, LOCAL_ROWS, LEVS, CHANNELS), jnp.float32),
            pltpu.VMEM((SLOTS, PLANES, LOCAL_ROWS, PER_PLANE, LEVS, CHANNELS), jnp.float32),
            pltpu.VMEM(final, jnp.float32),
            pltpu.SemaphoreType.DMA((2, SLOTS)),
            pltpu.SemaphoreType.DMA((3,)),
            pltpu.SemaphoreType.DMA((SLOTS,)),
            pltpu.SemaphoreType.DMA((SLOTS,)),
            pltpu.SemaphoreType.DMA((SLOTS,)),
            pltpu.SemaphoreType.DMA((3, SLOTS)),
            pltpu.SemaphoreType.DMA,
        ],
        compiler_params=pltpu.CompilerParams(
            collective_id=0, has_side_effects=True, vmem_limit_bytes=60 << 20
        ),
    )(wave_table, legendre_values, spectra)


def rows_kernel(longitudes_ref, waves_ref, arrived_ref, out_ref, turned, cos_sum, sin_sum):
    longitudes = longitudes_ref[pl.program_id(0)]
    period = (2 * longitudes).astype(jnp.float32)
    period_row = jnp.full((8, 128), period, jnp.float32)
    inverse = (jnp.float32(1.0) / period_row)[:1, :1]
    largest = lax.div(longitudes - 1, 2).astype(jnp.float32)
    odd = (2 * lax.broadcasted_iota(jnp.int32, (HALF, HALF), 1) + 1).astype(jnp.float32)
    centre = (
        2 * SPAN * lax.broadcasted_iota(jnp.int32, (16, HALF), 0) + (SPAN - 1)
    ).astype(jnp.float32)
    cos_sum[...] = jnp.zeros_like(cos_sum)
    sin_sum[...] = jnp.zeros_like(sin_sum)

    def slot_step(slot, carry):
        wave_row = waves_ref[pl.ds(slot, 1), :].astype(jnp.float32)
        wave_column = jnp.broadcast_to(wave_row, (HALF, HALF)).T
        table_cos, table_sin = cos_sin_of_turns(wave_column * odd, period, inverse)
        cos_high, cos_low = split(table_cos)
        sin_high, sin_low = split(table_sin)
        cos_table = jnp.concatenate([cos_high, cos_high, cos_low], axis=0)
        sin_table = jnp.concatenate([sin_high, sin_high, sin_low], axis=0)
        block_cos, block_sin = cos_sin_of_turns(wave_row * centre, period, inverse)
        weight = jnp.where(
            wave_row > largest,
            jnp.float32(0.0),
            jnp.where(wave_row == 0, jnp.float32(1.0), jnp.float32(2.0)),
        )
        values = arrived_ref[slot, 0].reshape(DEVICES, CHANNELS)
        for half in range(2):
            turned[half] = values[half * 128 : half * 128 + 128, :].T
        real, imag = (
            jnp.concatenate(
                [turned[half, pl.ds(part, FIELDS, stride=2), :] for half in range(2)], axis=1
            )
            * weight
            for part in range(2)
        )
        real_parts = []
        imag_parts = []
        for k in range(BLOCKS):
            c = block_cos[k : k + 1, :]
            s = block_sin[k : k + 1, :]
            high, low = split(real * c - imag * s)
            real_parts.append(jnp.concatenate([high, low, high], axis=1))
            high, low = split(real * s + imag * c)
            imag_parts.append(jnp.concatenate([high, low, high], axis=1))
        real_side = jnp.concatenate(real_parts, axis=0)
        imag_side = jnp.concatenate(imag_parts, axis=0)
        cos_sum[...] += jnp.dot(real_side, cos_table, preferred_element_type=jnp.float32)
        sin_sum[...] += jnp.dot(imag_side, sin_table, preferred_element_type=jnp.float32)
        return carry

    lax.fori_loop(0, SLOTS, slot_step, 0)
    backwards = 127 - lax.broadcasted_iota(jnp.int32, (FIELDS, 128), 1)
    column = lax.broadcasted_iota(jnp.int32, (FIELDS, 128), 1)
    for k in range(BLOCKS):
        rows = pl.ds(k * FIELDS, FIELDS)
        for part in range(2):
            lanes = pl.ds(part * 128, 128)
            c = cos_sum[rows, lanes]
            s = sin_sum[rows, lanes]
            first = k * SPAN + 128 * (1 - part)
            values = jnp.take_along_axis(c + s, backwards, axis=1)
            out_ref[0, :, pl.ds(first, 128)] = jnp.where(
                column + first < longitudes, values, jnp.float32(0.0)
            )
            first = k * SPAN + HALF + 128 * part
            if first < NLON:
                out_ref[0, :, pl.ds(first, 128)] = jnp.where(
                    column + first < longitudes, c - s, jnp.float32(0.0)
                )


def rows_transform(row_longitudes, waves, arrived, interpret=False):
    return pl.pallas_call(
        rows_kernel,
        out_shape=jax.ShapeDtypeStruct((LOCAL_ROWS, FIELDS, NLON), jnp.float32),
        grid=(LOCAL_ROWS,),
        in_specs=[
            pl.BlockSpec(memory_space=pltpu.SMEM),
            pl.BlockSpec(memory_space=pltpu.VMEM),
            pl.BlockSpec(
                (SLOTS, 1, PLANES, PER_PLANE, LEVS, CHANNELS), lambda r: (0, r, 0, 0, 0, 0)
            ),
        ],
        out_specs=pl.BlockSpec((1, FIELDS, NLON), lambda r: (r, 0, 0)),
        scratch_shapes=[
            pltpu.VMEM((2, CHANNELS, 128), jnp.float32),
            pltpu.VMEM((STACKED, HALF), jnp.float32),
            pltpu.VMEM((STACKED, HALF), jnp.float32),
        ],
        compiler_params=pltpu.CompilerParams(vmem_limit_bytes=60 << 20),
        interpret=interpret,
    )(row_longitudes, waves, arrived)


def per_device(legendre_values, spectra, wave_table, row_longitudes):
    waves = wave_table.reshape(DEVICES, SLOTS).T
    arrived = exchange(wave_table, legendre_values, spectra)
    return rows_transform(row_longitudes, waves, arrived)


def solution(mesh):
    in_specs = (
        P(("wave", "lev"), None, None),
        P(("wave", "lev"), None, None),
        P(),
        P(("wave", "lev")),
    )
    out_specs = P(("wave", "lev"), None, None)
    return jax.shard_map(
        per_device, mesh=mesh, in_specs=in_specs, out_specs=out_specs, check_vma=False
    )
```

```python
import jax
import jax.numpy as jnp
from jax import lax
from jax.experimental import pallas as pl
from jax.experimental.pallas import tpu as pltpu
from jax.sharding import PartitionSpec as P

MESH = pl.DeviceIdType.MESH

SLOTS = 5
SLOT_ORDER = (2, 0, 3, 1, 4)
DEGREES = 1280
ROWS = 512
CHANNELS = 128
FIELDS = 64
LOCAL_ROWS = 2
PLANES = 8
PER_PLANE = 4
WAVES = PLANES * PER_PLANE
LEVS = 8
DEVICES = WAVES * LEVS
NLON = 5376
HALF = 256
SPAN = 2 * HALF
BLOCKS = 11
STACKED = BLOCKS * FIELDS

COS_TERMS = (
    0.9999999996168156,
    -19.73920863354667,
    64.93938183835107,
    -85.4564814603686,
    60.24009011425828,
    -26.392650988301078,
    7.765225095262238,
    -1.4134373617596543,
)
SIN_TERMS = (
    6.283185293777215,
    -41.341697721207424,
    81.605000209223,
    -76.70070302960839,
    42.00769493017941,
    -14.834123486306066,
    3.1498534224128543,
)


def horner(terms, square):
    total = jnp.full_like(square, terms[-1])
    for term in terms[-2::-1]:
        total = total * square + jnp.float32(term)
    return total


def cos_sin_of_turns(product, period, inverse):
    whole = jnp.round(product * inverse)
    turn = (product - whole * period) * inverse
    square = turn * turn
    return horner(COS_TERMS, square), turn * horner(SIN_TERMS, square)


def split(values):
    high = values.astype(jnp.bfloat16)
    low = (values - high.astype(jnp.float32)).astype(jnp.bfloat16)
    return high, low


def transform_kernel(
    slot_waves_ref, longitudes_ref, waves_ref, legendre_ref, spectra_ref, out_ref,
    legendre, spectra, fourier, lev_first, x_second, z_first, x_after, final,
    columns, cos_tables, sin_tables, cos_turns, sin_turns, turned, cos_sum, sin_sum, grid,
    load_sem, send_sem, recv_sem, own_sem, out_sem,
):
    wave = lax.axis_index("wave")
    lev = lax.axis_index("lev")
    z, x = lax.div(wave, PER_PLANE), lax.rem(wave, PER_PLANE)
    me = wave * LEVS + lev
    lev_peers = [lax.rem(lev + k, LEVS) for k in range(1, LEVS)]
    x_peers = [lax.rem(x + k, PER_PLANE) for k in range(1, PER_PLANE)]
    z_peers = [lax.rem(z + k, PLANES) for k in (4, 3, 5, 2, 6, 1, 7)]

    def at_lev(peer):
        return wave, peer

    def at_x(peer):
        return z * PER_PLANE + peer, lev

    def at_z(peer):
        return peer * PER_PLANE + x, lev

    def load(slot):
        return (
            pltpu.make_async_copy(spectra_ref.at[slot], spectra.at[slot], load_sem.at[0, slot]),
            pltpu.make_async_copy(legendre_ref.at[slot], legendre.at[slot], load_sem.at[1, slot]),
        )

    for slot in SLOT_ORDER:
        for copy in load(slot):
            copy.start()

    barrier = pltpu.get_barrier_semaphore()
    for peers, at in ((z_peers, at_z), (x_peers, at_x), (lev_peers, at_lev)):
        for peer in peers:
            pl.semaphore_signal(barrier, inc=1, device_id=at(peer), device_id_type=MESH)

    degree = lax.broadcasted_iota(jnp.int32, (DEGREES, CHANNELS), 0)

    def legendre_step(slot):
        for copy in load(slot):
            copy.wait()
        wavenumber = slot_waves_ref[me * SLOTS + slot]
        values = spectra[slot].astype(jnp.float32)
        kept = jnp.where(degree >= wavenumber, values, jnp.float32(0.0)).astype(jnp.bfloat16)
        sums = jnp.dot(legendre[slot], kept, preferred_element_type=jnp.float32)
        fourier[slot] = sums.reshape(WAVES, LEVS * LOCAL_ROWS, CHANNELS)

    def move(stage, slot, source, target, peers, own, at):
        for peer in peers:
            pltpu.make_async_remote_copy(
                src_ref=source(peer),
                dst_ref=target,
                send_sem=send_sem.at[stage],
                recv_sem=recv_sem.at[stage, slot],
                device_id=at(peer),
                device_id_type=MESH,
            ).start()
        pltpu.make_async_copy(source(own), target, own_sem.at[stage, slot]).start()

    def arrived(stage, slot):
        count = 24 if stage == 1 else 28
        region = final.at[slot, pl.ds(0, count)]
        pltpu.make_async_copy(region, region, recv_sem.at[stage, slot]).wait()
        region = final.at[slot, pl.ds(0, WAVES - count)]
        pltpu.make_async_copy(region, region, own_sem.at[stage, slot]).wait()

    def pair(peer):
        return pl.ds(peer * LOCAL_ROWS, LOCAL_ROWS)

    def plane(peer):
        return pl.ds(peer * PER_PLANE, PER_PLANE)

    def first_move(slot):
        if slot < 2:
            move(
                0, slot, lambda peer: fourier.at[slot, plane(peer)],
                z_first.at[slot, z], z_peers, z, at_z,
            )
        else:
            move(
                0, slot, lambda peer: fourier.at[slot, :, pair(peer), :],
                lev_first.at[slot - 2, :, :, lev, :], lev_peers, lev, at_lev,
            )

    def second_move(slot):
        arrived(0, slot)
        if slot < 2:
            move(
                1, slot, lambda peer: z_first.at[slot, :, peer],
                x_after.at[slot, :, x], x_peers, x, at_x,
            )
        else:
            move(
                1, slot,
                lambda peer: lev_first.at[slot - 2].reshape(
                    PLANES, PER_PLANE, LOCAL_ROWS, LEVS, CHANNELS
                ).at[:, peer],
                x_second.at[slot - 2, :, x], x_peers, x, at_x,
            )

    def last_move(slot):
        arrived(1, slot)
        if slot < 2:
            move(
                2, slot,
                lambda peer: x_after.at[slot].reshape(
                    WAVES, LEVS * LOCAL_ROWS, CHANNELS
                ).at[:, pair(peer), :],
                final.at[slot, :, :, lev, :], lev_peers, lev, at_lev,
            )
        else:
            move(
                2, slot, lambda peer: x_second.at[slot - 2, peer],
                final.at[slot, plane(z)], z_peers, z, at_z,
            )

    odd = (2 * lax.broadcasted_iota(jnp.int32, (HALF, HALF), 1) + 1).astype(jnp.float32)
    centre = (
        2 * SPAN * lax.broadcasted_iota(jnp.int32, (16, HALF), 0) + (SPAN - 1)
    ).astype(jnp.float32)

    def spread_waves():
        for part in range(SLOTS * DEVICES // 128):
            row = waves_ref[pl.ds(part, 1), :].astype(jnp.float32)
            columns[pl.ds(part * 128, 128), :] = jnp.broadcast_to(row, (128, 128)).T

    def table_step(row, slot):
        longitudes = longitudes_ref[row]
        period = (2 * longitudes).astype(jnp.float32)
        inverse = (jnp.float32(1.0) / jnp.full((8, 128), period, jnp.float32))[:1, :1]
        largest = lax.div(longitudes - 1, 2).astype(jnp.float32)
        wave_column = columns[pl.ds(slot, DEVICES, stride=SLOTS), :]
        wave_row = jnp.concatenate([wave_column[:128, :].T, wave_column[128:, :].T], axis=1)[:16, :]
        product = jnp.concatenate([wave_column, wave_column], axis=1) * odd
        table_cos, table_sin = cos_sin_of_turns(product, period, inverse)
        for table, tables in ((table_cos, cos_tables), (table_sin, sin_tables)):
            high, low = split(table)
            tables[slot, row, pl.ds(0, HALF), :] = high
            tables[slot, row, pl.ds(HALF, HALF), :] = high
            tables[slot, row, pl.ds(2 * HALF, HALF), :] = low
        weight = jnp.where(
            wave_row > largest,
            jnp.float32(0.0),
            jnp.where(wave_row == 0, jnp.float32(1.0), jnp.float32(2.0)),
        )
        block_cos, block_sin = cos_sin_of_turns(wave_row * centre, period, inverse)
        cos_turns[slot, row] = block_cos * weight
        sin_turns[slot, row] = block_sin * weight

    def add_step(slot, row):
        values = final[slot, :, row].reshape(DEVICES, CHANNELS)
        for half in range(2):
            turned[half] = values[half * 128 : half * 128 + 128, :].T
        real, imag = (
            jnp.concatenate(
                [turned[half, pl.ds(part, FIELDS, stride=2), :] for half in range(2)], axis=1
            )
            for part in range(2)
        )
        block_cos = cos_turns[slot, row]
        block_sin = sin_turns[slot, row]
        real_parts = []
        imag_parts = []
        for k in range(BLOCKS):
            c = block_cos[k : k + 1, :]
            s = block_sin[k : k + 1, :]
            high, low = split(real * c - imag * s)
            real_parts.append(jnp.concatenate([high, low, high], axis=1))
            high, low = split(real * s + imag * c)
            imag_parts.append(jnp.concatenate([high, low, high], axis=1))
        real_side = jnp.concatenate(real_parts, axis=0)
        imag_side = jnp.concatenate(imag_parts, axis=0)
        cos_sum[row] += jnp.dot(
            real_side, cos_tables[slot, row], preferred_element_type=jnp.float32
        )
        sin_sum[row] += jnp.dot(
            imag_side, sin_tables[slot, row], preferred_element_type=jnp.float32
        )

    backwards = 127 - lax.broadcasted_iota(jnp.int32, (FIELDS, 128), 1)
    column = lax.broadcasted_iota(jnp.int32, (FIELDS, 128), 1)

    def finish(row):
        longitudes = longitudes_ref[row]
        for k in range(BLOCKS):
            rows = pl.ds(k * FIELDS, FIELDS)
            for part in range(2):
                lanes = pl.ds(part * 128, 128)
                c = cos_sum[row, rows, lanes]
                s = sin_sum[row, rows, lanes]
                first = k * SPAN + 128 * (1 - part)
                values = jnp.take_along_axis(c + s, backwards, axis=1)
                grid[row, :, pl.ds(first, 128)] = jnp.where(
                    column + first < longitudes, values, jnp.float32(0.0)
                )
                first = k * SPAN + HALF + 128 * part
                if first < NLON:
                    grid[row, :, pl.ds(first, 128)] = jnp.where(
                        column + first < longitudes, c - s, jnp.float32(0.0)
                    )

    def loop(count, act):
        def step(i, carry):
            act(i)
            return carry

        lax.fori_loop(0, count, step, 0)

    legendre_step(SLOT_ORDER[0])
    pl.semaphore_wait(barrier, LEVS + PER_PLANE + PLANES - 3)
    first_move(SLOT_ORDER[0])
    for slot in SLOT_ORDER[1:]:
        legendre_step(slot)
        first_move(slot)
    spread_waves()
    for row in range(LOCAL_ROWS):
        cos_sum[row] = jnp.zeros((STACKED, HALF), jnp.float32)
        sin_sum[row] = jnp.zeros((STACKED, HALF), jnp.float32)
    second_move(2)
    second_move(3)
    loop(SLOTS, lambda slot: table_step(0, slot))
    second_move(0)
    second_move(4)
    last_move(2)
    last_move(3)
    last_move(4)
    loop(SLOTS, lambda slot: table_step(1, slot))
    last_move(0)
    second_move(1)
    last_move(1)

    def slot_step(slot):
        arrived(2, slot)
        loop(LOCAL_ROWS, lambda row: add_step(slot, row))

    loop(SLOTS, slot_step)
    for row in range(LOCAL_ROWS):
        finish(row)
        pltpu.make_async_copy(grid.at[row], out_ref.at[row], out_sem).start()
    for stage in range(3):
        region = final.at[:, pl.ds(0, 24 if stage == 1 else 28)]
        pltpu.make_async_copy(region, region, send_sem.at[stage]).wait()
    pltpu.make_async_copy(grid, out_ref, out_sem).wait()


def transform(wave_table, row_longitudes, legendre_values, spectra):
    hbm = pl.BlockSpec(memory_space=pltpu.HBM)
    smem = pl.BlockSpec(memory_space=pltpu.SMEM)
    tables = pltpu.VMEM((SLOTS, LOCAL_ROWS, 3 * HALF, HALF), jnp.bfloat16)
    turns = pltpu.VMEM((SLOTS, LOCAL_ROWS, 16, HALF), jnp.float32)
    sums = pltpu.VMEM((LOCAL_ROWS, STACKED, HALF), jnp.float32)
    z_then_x = pltpu.VMEM((2, PLANES, PER_PLANE, LEVS * LOCAL_ROWS, CHANNELS), jnp.float32)
    return pl.pallas_call(
        transform_kernel,
        out_shape=jax.ShapeDtypeStruct((LOCAL_ROWS, FIELDS, NLON), jnp.float32),
        in_specs=[smem, smem, pl.BlockSpec(memory_space=pltpu.VMEM), hbm, hbm],
        out_specs=pl.BlockSpec(memory_space=pl.ANY),
        scratch_shapes=[
            pltpu.VMEM((SLOTS, ROWS, DEGREES), jnp.bfloat16),
            pltpu.VMEM((SLOTS, DEGREES, CHANNELS), jnp.bfloat16),
            pltpu.VMEM((SLOTS, WAVES, LEVS * LOCAL_ROWS, CHANNELS), jnp.float32),
            pltpu.VMEM((3, WAVES, LOCAL_ROWS, LEVS, CHANNELS), jnp.float32),
            pltpu.VMEM((3, PLANES, PER_PLANE, LOCAL_ROWS, LEVS, CHANNELS), jnp.float32),
            z_then_x,
            z_then_x,
            pltpu.VMEM((SLOTS, WAVES, LOCAL_ROWS, LEVS, CHANNELS), jnp.float32),
            pltpu.VMEM((SLOTS * DEVICES, 128), jnp.float32),
            tables,
            tables,
            turns,
            turns,
            pltpu.VMEM((2, CHANNELS, 128), jnp.float32),
            sums,
            sums,
            pltpu.VMEM((LOCAL_ROWS, FIELDS, NLON), jnp.float32),
            pltpu.SemaphoreType.DMA((2, SLOTS)),
            pltpu.SemaphoreType.DMA((3,)),
            pltpu.SemaphoreType.DMA((3, SLOTS)),
            pltpu.SemaphoreType.DMA((3, SLOTS)),
            pltpu.SemaphoreType.DMA,
        ],
        compiler_params=pltpu.CompilerParams(
            collective_id=0, has_side_effects=True, vmem_limit_bytes=48 << 20
        ),
    )(
        wave_table,
        row_longitudes,
        wave_table.reshape(SLOTS * DEVICES // 128, 128),
        legendre_values,
        spectra,
    )


def per_device(legendre_values, spectra, wave_table, row_longitudes):
    return transform(wave_table, row_longitudes, legendre_values, spectra)


def solution(mesh):
    in_specs = (
        P(("wave", "lev"), None, None),
        P(("wave", "lev"), None, None),
        P(),
        P(("wave", "lev")),
    )
    out_specs = P(("wave", "lev"), None, None)
    return jax.shard_map(
        per_device, mesh=mesh, in_specs=in_specs, out_specs=out_specs, check_vma=False
    )
```

```python
import jax
import jax.numpy as jnp
from jax import lax
from jax.experimental import pallas as pl
from jax.experimental.pallas import tpu as pltpu
from jax.sharding import PartitionSpec as P

MESH = pl.DeviceIdType.MESH

SLOTS = 5
DEGREES = 1280
ROWS = 512
CHANNELS = 128
FIELDS = 64
LOCAL_ROWS = 2
PLANES = 8
PER_PLANE = 4
WAVES = PLANES * PER_PLANE
LEVS = 8
DEVICES = WAVES * LEVS
NLON = 5376
HALF = 256
SPAN = 2 * HALF
BLOCKS = 11
STACKED = BLOCKS * FIELDS

COS_TERMS = (
    0.9999999996168156,
    -19.73920863354667,
    64.93938183835107,
    -85.4564814603686,
    60.24009011425828,
    -26.392650988301078,
    7.765225095262238,
    -1.4134373617596543,
)
SIN_TERMS = (
    6.283185293777215,
    -41.341697721207424,
    81.605000209223,
    -76.70070302960839,
    42.00769493017941,
    -14.834123486306066,
    3.1498534224128543,
)


def horner(terms, square):
    total = jnp.full_like(square, terms[-1])
    for term in terms[-2::-1]:
        total = total * square + jnp.float32(term)
    return total


def cos_sin_of_turns(product, period, inverse):
    whole = jnp.round(product * inverse)
    turn = (product - whole * period) * inverse
    square = turn * turn
    return horner(COS_TERMS, square), turn * horner(SIN_TERMS, square)


def split(values):
    high = values.astype(jnp.bfloat16)
    low = (values - high.astype(jnp.float32)).astype(jnp.bfloat16)
    return high, low


def transform_kernel(
    slot_waves_ref, longitudes_ref, waves_ref, legendre_ref, spectra_ref, out_ref,
    legendre, spectra, fourier, lev_first, x_second, z_first, x_after, final,
    columns, cos_tables, sin_tables, cos_turns, sin_turns, turned, cos_sum, sin_sum, grid,
    load_sem, send_sem, recv_sem, own_sem, out_sem,
):
    wave = lax.axis_index("wave")
    lev = lax.axis_index("lev")
    z, x = lax.div(wave, PER_PLANE), lax.rem(wave, PER_PLANE)
    me = wave * LEVS + lev
    lev_peers = [lax.rem(lev + k, LEVS) for k in range(1, LEVS)]
    x_peers = [lax.rem(x + k, PER_PLANE) for k in range(1, PER_PLANE)]
    z_peers = [lax.rem(z + k, PLANES) for k in (4, 3, 5, 2, 6, 1, 7)]

    def at_lev(peer):
        return wave, peer

    def at_x(peer):
        return z * PER_PLANE + peer, lev

    def at_z(peer):
        return peer * PER_PLANE + x, lev

    def load(slot):
        return (
            pltpu.make_async_copy(spectra_ref.at[slot], spectra.at[slot], load_sem.at[0, slot]),
            pltpu.make_async_copy(legendre_ref.at[slot], legendre.at[slot], load_sem.at[1, slot]),
        )

    for slot in range(SLOTS):
        for copy in load(slot):
            copy.start()

    barrier = pltpu.get_barrier_semaphore()
    for peers, at in ((z_peers, at_z), (x_peers, at_x), (lev_peers, at_lev)):
        for peer in peers:
            pl.semaphore_signal(barrier, inc=1, device_id=at(peer), device_id_type=MESH)

    degree = lax.broadcasted_iota(jnp.int32, (DEGREES, CHANNELS), 0)

    def legendre_step(slot):
        for copy in load(slot):
            copy.wait()
        wavenumber = slot_waves_ref[me * SLOTS + slot]
        values = spectra[slot].astype(jnp.float32)
        kept = jnp.where(degree >= wavenumber, values, jnp.float32(0.0)).astype(jnp.bfloat16)
        sums = jnp.dot(legendre[slot], kept, preferred_element_type=jnp.float32)
        fourier[slot] = sums.reshape(WAVES, LEVS * LOCAL_ROWS, CHANNELS)

    def move(stage, slot, source, target, peers, own, at):
        for peer in peers:
            pltpu.make_async_remote_copy(
                src_ref=source(peer),
                dst_ref=target,
                send_sem=send_sem.at[stage],
                recv_sem=recv_sem.at[stage, slot],
                device_id=at(peer),
                device_id_type=MESH,
            ).start()
        pltpu.make_async_copy(source(own), target, own_sem.at[stage, slot]).start()

    def arrived(stage, slot):
        count = 24 if stage == 1 else 28
        region = final.at[slot, pl.ds(0, count)]
        pltpu.make_async_copy(region, region, recv_sem.at[stage, slot]).wait()
        region = final.at[slot, pl.ds(0, WAVES - count)]
        pltpu.make_async_copy(region, region, own_sem.at[stage, slot]).wait()

    def pair(peer):
        return pl.ds(peer * LOCAL_ROWS, LOCAL_ROWS)

    def plane(peer):
        return pl.ds(peer * PER_PLANE, PER_PLANE)

    def first_move(slot):
        if slot % 2:
            move(
                0, slot, lambda peer: fourier.at[slot, plane(peer)],
                z_first.at[slot // 2, z], z_peers, z, at_z,
            )
        else:
            move(
                0, slot, lambda peer: fourier.at[slot, :, pair(peer), :],
                lev_first.at[slot // 2, :, :, lev, :], lev_peers, lev, at_lev,
            )

    def second_move(slot):
        arrived(0, slot)
        if slot % 2:
            move(
                1, slot, lambda peer: z_first.at[slot // 2, :, peer],
                x_after.at[slot // 2, :, x], x_peers, x, at_x,
            )
        else:
            move(
                1, slot,
                lambda peer: lev_first.at[slot // 2].reshape(
                    PLANES, PER_PLANE, LOCAL_ROWS, LEVS, CHANNELS
                ).at[:, peer],
                x_second.at[slot // 2, :, x], x_peers, x, at_x,
            )

    def last_move(slot):
        arrived(1, slot)
        if slot % 2:
            move(
                2, slot,
                lambda peer: x_after.at[slot // 2].reshape(
                    WAVES, LEVS * LOCAL_ROWS, CHANNELS
                ).at[:, pair(peer), :],
                final.at[slot, :, :, lev, :], lev_peers, lev, at_lev,
            )
        else:
            move(
                2, slot, lambda peer: x_second.at[slot // 2, peer],
                final.at[slot, plane(z)], z_peers, z, at_z,
            )

    odd = (2 * lax.broadcasted_iota(jnp.int32, (HALF, HALF), 1) + 1).astype(jnp.float32)
    centre = (
        2 * SPAN * lax.broadcasted_iota(jnp.int32, (16, HALF), 0) + (SPAN - 1)
    ).astype(jnp.float32)

    def spread_waves():
        for part in range(SLOTS * DEVICES // 128):
            row = waves_ref[pl.ds(part, 1), :].astype(jnp.float32)
            columns[pl.ds(part * 128, 128), :] = jnp.broadcast_to(row, (128, 128)).T

    def table_step(row, slot):
        longitudes = longitudes_ref[row]
        period = (2 * longitudes).astype(jnp.float32)
        inverse = (jnp.float32(1.0) / jnp.full((8, 128), period, jnp.float32))[:1, :1]
        largest = lax.div(longitudes - 1, 2).astype(jnp.float32)
        wave_column = columns[pl.ds(slot, DEVICES, stride=SLOTS), :]
        wave_row = jnp.concatenate([wave_column[:128, :].T, wave_column[128:, :].T], axis=1)[:16, :]
        product = jnp.concatenate([wave_column, wave_column], axis=1) * odd
        table_cos, table_sin = cos_sin_of_turns(product, period, inverse)
        for table, tables in ((table_cos, cos_tables), (table_sin, sin_tables)):
            high, low = split(table)
            tables[slot, row, pl.ds(0, HALF), :] = high
            tables[slot, row, pl.ds(HALF, HALF), :] = high
            tables[slot, row, pl.ds(2 * HALF, HALF), :] = low
        weight = jnp.where(
            wave_row > largest,
            jnp.float32(0.0),
            jnp.where(wave_row == 0, jnp.float32(1.0), jnp.float32(2.0)),
        )
        block_cos, block_sin = cos_sin_of_turns(wave_row * centre, period, inverse)
        cos_turns[slot, row] = block_cos * weight
        sin_turns[slot, row] = block_sin * weight

    def add_step(slot, row):
        values = final[slot, :, row].reshape(DEVICES, CHANNELS)
        for half in range(2):
            turned[half] = values[half * 128 : half * 128 + 128, :].T
        real, imag = (
            jnp.concatenate(
                [turned[half, pl.ds(part, FIELDS, stride=2), :] for half in range(2)], axis=1
            )
            for part in range(2)
        )
        block_cos = cos_turns[slot, row]
        block_sin = sin_turns[slot, row]
        real_parts = []
        imag_parts = []
        for k in range(BLOCKS):
            c = block_cos[k : k + 1, :]
            s = block_sin[k : k + 1, :]
            high, low = split(real * c - imag * s)
            real_parts.append(jnp.concatenate([high, low, high], axis=1))
            high, low = split(real * s + imag * c)
            imag_parts.append(jnp.concatenate([high, low, high], axis=1))
        real_side = jnp.concatenate(real_parts, axis=0)
        imag_side = jnp.concatenate(imag_parts, axis=0)
        cos_sum[row] += jnp.dot(
            real_side, cos_tables[slot, row], preferred_element_type=jnp.float32
        )
        sin_sum[row] += jnp.dot(
            imag_side, sin_tables[slot, row], preferred_element_type=jnp.float32
        )

    backwards = 127 - lax.broadcasted_iota(jnp.int32, (FIELDS, 128), 1)
    column = lax.broadcasted_iota(jnp.int32, (FIELDS, 128), 1)

    def finish(row):
        longitudes = longitudes_ref[row]
        for k in range(BLOCKS):
            rows = pl.ds(k * FIELDS, FIELDS)
            for part in range(2):
                lanes = pl.ds(part * 128, 128)
                c = cos_sum[row, rows, lanes]
                s = sin_sum[row, rows, lanes]
                first = k * SPAN + 128 * (1 - part)
                values = jnp.take_along_axis(c + s, backwards, axis=1)
                grid[row, :, pl.ds(first, 128)] = jnp.where(
                    column + first < longitudes, values, jnp.float32(0.0)
                )
                first = k * SPAN + HALF + 128 * part
                if first < NLON:
                    grid[row, :, pl.ds(first, 128)] = jnp.where(
                        column + first < longitudes, c - s, jnp.float32(0.0)
                    )

    def loop(count, act):
        def step(i, carry):
            act(i)
            return carry

        lax.fori_loop(0, count, step, 0)

    legendre_step(0)
    pl.semaphore_wait(barrier, LEVS + PER_PLANE + PLANES - 3)
    first_move(0)
    for slot in range(1, SLOTS):
        legendre_step(slot)
        first_move(slot)
    spread_waves()
    for row in range(LOCAL_ROWS):
        cos_sum[row] = jnp.zeros((STACKED, HALF), jnp.float32)
        sin_sum[row] = jnp.zeros((STACKED, HALF), jnp.float32)
    second_move(0)
    second_move(2)
    loop(SLOTS, lambda slot: table_step(0, slot))
    second_move(1)
    second_move(4)
    last_move(0)
    last_move(2)
    second_move(3)
    last_move(4)
    last_move(1)
    loop(SLOTS, lambda slot: table_step(1, slot))
    last_move(3)

    def slot_step(slot):
        arrived(2, slot)
        loop(LOCAL_ROWS, lambda row: add_step(slot, row))

    loop(SLOTS, slot_step)
    for row in range(LOCAL_ROWS):
        finish(row)
        pltpu.make_async_copy(grid.at[row], out_ref.at[row], out_sem).start()
    for stage in range(3):
        region = final.at[:, pl.ds(0, 24 if stage == 1 else 28)]
        pltpu.make_async_copy(region, region, send_sem.at[stage]).wait()
    pltpu.make_async_copy(grid, out_ref, out_sem).wait()


def transform(wave_table, row_longitudes, legendre_values, spectra):
    hbm = pl.BlockSpec(memory_space=pltpu.HBM)
    smem = pl.BlockSpec(memory_space=pltpu.SMEM)
    tables = pltpu.VMEM((SLOTS, LOCAL_ROWS, 3 * HALF, HALF), jnp.bfloat16)
    turns = pltpu.VMEM((SLOTS, LOCAL_ROWS, 16, HALF), jnp.float32)
    sums = pltpu.VMEM((LOCAL_ROWS, STACKED, HALF), jnp.float32)
    z_then_x = pltpu.VMEM((2, PLANES, PER_PLANE, LEVS * LOCAL_ROWS, CHANNELS), jnp.float32)
    return pl.pallas_call(
        transform_kernel,
        out_shape=jax.ShapeDtypeStruct((LOCAL_ROWS, FIELDS, NLON), jnp.float32),
        in_specs=[smem, smem, pl.BlockSpec(memory_space=pltpu.VMEM), hbm, hbm],
        out_specs=pl.BlockSpec(memory_space=pl.ANY),
        scratch_shapes=[
            pltpu.VMEM((SLOTS, ROWS, DEGREES), jnp.bfloat16),
            pltpu.VMEM((SLOTS, DEGREES, CHANNELS), jnp.bfloat16),
            pltpu.VMEM((SLOTS, WAVES, LEVS * LOCAL_ROWS, CHANNELS), jnp.float32),
            pltpu.VMEM((3, WAVES, LOCAL_ROWS, LEVS, CHANNELS), jnp.float32),
            pltpu.VMEM((3, PLANES, PER_PLANE, LOCAL_ROWS, LEVS, CHANNELS), jnp.float32),
            z_then_x,
            z_then_x,
            pltpu.VMEM((SLOTS, WAVES, LOCAL_ROWS, LEVS, CHANNELS), jnp.float32),
            pltpu.VMEM((SLOTS * DEVICES, 128), jnp.float32),
            tables,
            tables,
            turns,
            turns,
            pltpu.VMEM((2, CHANNELS, 128), jnp.float32),
            sums,
            sums,
            pltpu.VMEM((LOCAL_ROWS, FIELDS, NLON), jnp.float32),
            pltpu.SemaphoreType.DMA((2, SLOTS)),
            pltpu.SemaphoreType.DMA((3,)),
            pltpu.SemaphoreType.DMA((3, SLOTS)),
            pltpu.SemaphoreType.DMA((3, SLOTS)),
            pltpu.SemaphoreType.DMA,
        ],
        compiler_params=pltpu.CompilerParams(
            collective_id=0, has_side_effects=True, vmem_limit_bytes=48 << 20
        ),
    )(
        *(
            pltpu.with_memory_space_constraint(operand, pltpu.HBM)
            for operand in (
                wave_table,
                row_longitudes,
                wave_table.reshape(SLOTS * DEVICES // 128, 128),
                legendre_values,
                spectra,
            )
        )
    )


def per_device(legendre_values, spectra, wave_table, row_longitudes):
    return transform(wave_table, row_longitudes, legendre_values, spectra)


def solution(mesh):
    in_specs = (
        P(("wave", "lev"), None, None),
        P(("wave", "lev"), None, None),
        P(),
        P(("wave", "lev")),
    )
    out_specs = P(("wave", "lev"), None, None)
    return jax.shard_map(
        per_device, mesh=mesh, in_specs=in_specs, out_specs=out_specs, check_vma=False
    )
```

```python
import jax
import jax.numpy as jnp
from jax import lax
from jax.experimental import pallas as pl
from jax.experimental.pallas import tpu as pltpu
from jax.sharding import PartitionSpec as P

MESH = pl.DeviceIdType.MESH

SLOTS = 5
DEGREES = 1280
ROWS = 512
CHANNELS = 128
FIELDS = 64
LOCAL_ROWS = 2
PLANES = 8
PER_PLANE = 4
WAVES = PLANES * PER_PLANE
LEVS = 8
DEVICES = WAVES * LEVS
NLON = 5376
HALF = 256
SPAN = 2 * HALF
BLOCKS = 11
STACKED = BLOCKS * FIELDS

COS_TERMS = (
    0.9999999996168156,
    -19.73920863354667,
    64.93938183835107,
    -85.4564814603686,
    60.24009011425828,
    -26.392650988301078,
    7.765225095262238,
    -1.4134373617596543,
)
SIN_TERMS = (
    6.283185293777215,
    -41.341697721207424,
    81.605000209223,
    -76.70070302960839,
    42.00769493017941,
    -14.834123486306066,
    3.1498534224128543,
)


def horner(terms, square):
    total = jnp.full_like(square, terms[-1])
    for term in terms[-2::-1]:
        total = total * square + jnp.float32(term)
    return total


def cos_sin_of_turns(product, period, inverse):
    whole = jnp.round(product * inverse)
    turn = (product - whole * period) * inverse
    square = turn * turn
    return horner(COS_TERMS, square), turn * horner(SIN_TERMS, square)


def split(values):
    high = values.astype(jnp.bfloat16)
    low = (values - high.astype(jnp.float32)).astype(jnp.bfloat16)
    return high, low


def transform_kernel(
    slot_waves_ref, longitudes_ref, waves_ref, legendre_ref, spectra_ref, out_ref,
    legendre, spectra, fourier, lev_first, x_second, z_first, x_after, final,
    columns, cos_tables, sin_tables, cos_turns, sin_turns, turned, cos_sum, sin_sum,
    load_sem, send_sem, recv_sem, own_sem,
):
    wave = lax.axis_index("wave")
    lev = lax.axis_index("lev")
    z, x = lax.div(wave, PER_PLANE), lax.rem(wave, PER_PLANE)
    me = wave * LEVS + lev
    lev_peers = [lax.rem(lev + k, LEVS) for k in range(1, LEVS)]
    x_peers = [lax.rem(x + k, PER_PLANE) for k in range(1, PER_PLANE)]
    z_peers = [lax.rem(z + k, PLANES) for k in (4, 3, 5, 2, 6, 1, 7)]

    def at_lev(peer):
        return wave, peer

    def at_x(peer):
        return z * PER_PLANE + peer, lev

    def at_z(peer):
        return peer * PER_PLANE + x, lev

    def load(slot):
        return (
            pltpu.make_async_copy(spectra_ref.at[slot], spectra.at[slot], load_sem.at[0, slot]),
            pltpu.make_async_copy(legendre_ref.at[slot], legendre.at[slot], load_sem.at[1, slot]),
        )

    for slot in range(SLOTS):
        for copy in load(slot):
            copy.start()

    barrier = pltpu.get_barrier_semaphore()
    for peers, at in ((z_peers, at_z), (x_peers, at_x), (lev_peers, at_lev)):
        for peer in peers:
            pl.semaphore_signal(barrier, inc=1, device_id=at(peer), device_id_type=MESH)

    degree = lax.broadcasted_iota(jnp.int32, (DEGREES, CHANNELS), 0)

    def legendre_step(slot):
        for copy in load(slot):
            copy.wait()
        wavenumber = slot_waves_ref[me * SLOTS + slot]
        values = spectra[slot].astype(jnp.float32)
        kept = jnp.where(degree >= wavenumber, values, jnp.float32(0.0)).astype(jnp.bfloat16)
        sums = jnp.dot(legendre[slot], kept, preferred_element_type=jnp.float32)
        fourier[slot] = sums.reshape(WAVES, LEVS * LOCAL_ROWS, CHANNELS)

    def move(stage, slot, source, target, peers, own, at):
        for peer in peers:
            pltpu.make_async_remote_copy(
                src_ref=source(peer),
                dst_ref=target,
                send_sem=send_sem.at[stage],
                recv_sem=recv_sem.at[stage, slot],
                device_id=at(peer),
                device_id_type=MESH,
            ).start()
        pltpu.make_async_copy(source(own), target, own_sem.at[stage, slot]).start()

    def arrived(stage, slot):
        count = 24 if stage == 1 else 28
        region = final.at[slot, pl.ds(0, count)]
        pltpu.make_async_copy(region, region, recv_sem.at[stage, slot]).wait()
        region = final.at[slot, pl.ds(0, WAVES - count)]
        pltpu.make_async_copy(region, region, own_sem.at[stage, slot]).wait()

    def pair(peer):
        return pl.ds(peer * LOCAL_ROWS, LOCAL_ROWS)

    def plane(peer):
        return pl.ds(peer * PER_PLANE, PER_PLANE)

    def first_move(slot):
        if slot % 2:
            move(
                0, slot, lambda peer: fourier.at[slot, plane(peer)],
                z_first.at[slot // 2, z], z_peers, z, at_z,
            )
        else:
            move(
                0, slot, lambda peer: fourier.at[slot, :, pair(peer), :],
                lev_first.at[slot // 2, :, :, lev, :], lev_peers, lev, at_lev,
            )

    def second_move(slot):
        arrived(0, slot)
        if slot % 2:
            move(
                1, slot, lambda peer: z_first.at[slot // 2, :, peer],
                x_after.at[slot // 2, :, x], x_peers, x, at_x,
            )
        else:
            move(
                1, slot,
                lambda peer: lev_first.at[slot // 2].reshape(
                    PLANES, PER_PLANE, LOCAL_ROWS, LEVS, CHANNELS
                ).at[:, peer],
                x_second.at[slot // 2, :, x], x_peers, x, at_x,
            )

    def last_move(slot):
        arrived(1, slot)
        if slot % 2:
            move(
                2, slot,
                lambda peer: x_after.at[slot // 2].reshape(
                    WAVES, LEVS * LOCAL_ROWS, CHANNELS
                ).at[:, pair(peer), :],
                final.at[slot, :, :, lev, :], lev_peers, lev, at_lev,
            )
        else:
            move(
                2, slot, lambda peer: x_second.at[slot // 2, peer],
                final.at[slot, plane(z)], z_peers, z, at_z,
            )

    odd = (2 * lax.broadcasted_iota(jnp.int32, (HALF, HALF), 1) + 1).astype(jnp.float32)
    centre = (
        2 * SPAN * lax.broadcasted_iota(jnp.int32, (16, HALF), 0) + (SPAN - 1)
    ).astype(jnp.float32)

    def spread_waves():
        for part in range(SLOTS * DEVICES // 128):
            row = waves_ref[pl.ds(part, 1), :].astype(jnp.float32)
            columns[pl.ds(part * 128, 128), :] = jnp.broadcast_to(row, (128, 128)).T

    def table_step(row, slot):
        longitudes = longitudes_ref[row]
        period = (2 * longitudes).astype(jnp.float32)
        inverse = (jnp.float32(1.0) / jnp.full((8, 128), period, jnp.float32))[:1, :1]
        largest = lax.div(longitudes - 1, 2).astype(jnp.float32)
        wave_column = columns[pl.ds(slot, DEVICES, stride=SLOTS), :]
        wave_row = jnp.concatenate([wave_column[:128, :].T, wave_column[128:, :].T], axis=1)[:16, :]
        product = jnp.concatenate([wave_column, wave_column], axis=1) * odd
        table_cos, table_sin = cos_sin_of_turns(product, period, inverse)
        for table, tables in ((table_cos, cos_tables), (table_sin, sin_tables)):
            high, low = split(table)
            tables[slot, row, pl.ds(0, HALF), :] = high
            tables[slot, row, pl.ds(HALF, HALF), :] = high
            tables[slot, row, pl.ds(2 * HALF, HALF), :] = low
        weight = jnp.where(
            wave_row > largest,
            jnp.float32(0.0),
            jnp.where(wave_row == 0, jnp.float32(1.0), jnp.float32(2.0)),
        )
        block_cos, block_sin = cos_sin_of_turns(wave_row * centre, period, inverse)
        cos_turns[slot, row] = block_cos * weight
        sin_turns[slot, row] = block_sin * weight

    def add_step(slot, row):
        values = final[slot, :, row].reshape(DEVICES, CHANNELS)
        for half in range(2):
            turned[half] = values[half * 128 : half * 128 + 128, :].T
        real, imag = (
            jnp.concatenate(
                [turned[half, pl.ds(part, FIELDS, stride=2), :] for half in range(2)], axis=1
            )
            for part in range(2)
        )
        block_cos = cos_turns[slot, row]
        block_sin = sin_turns[slot, row]
        real_parts = []
        imag_parts = []
        for k in range(BLOCKS):
            c = block_cos[k : k + 1, :]
            s = block_sin[k : k + 1, :]
            high, low = split(real * c - imag * s)
            real_parts.append(jnp.concatenate([high, low, high], axis=1))
            high, low = split(real * s + imag * c)
            imag_parts.append(jnp.concatenate([high, low, high], axis=1))
        real_side = jnp.concatenate(real_parts, axis=0)
        imag_side = jnp.concatenate(imag_parts, axis=0)
        cos_sum[row] += jnp.dot(
            real_side, cos_tables[slot, row], preferred_element_type=jnp.float32
        )
        sin_sum[row] += jnp.dot(
            imag_side, sin_tables[slot, row], preferred_element_type=jnp.float32
        )

    backwards = 127 - lax.broadcasted_iota(jnp.int32, (FIELDS, 128), 1)
    column = lax.broadcasted_iota(jnp.int32, (FIELDS, 128), 1)

    def finish(row):
        longitudes = longitudes_ref[row]
        for k in range(BLOCKS):
            rows = pl.ds(k * FIELDS, FIELDS)
            for part in range(2):
                lanes = pl.ds(part * 128, 128)
                c = cos_sum[row, rows, lanes]
                s = sin_sum[row, rows, lanes]
                first = k * SPAN + 128 * (1 - part)
                values = jnp.take_along_axis(c + s, backwards, axis=1)
                out_ref[row, :, pl.ds(first, 128)] = jnp.where(
                    column + first < longitudes, values, jnp.float32(0.0)
                )
                first = k * SPAN + HALF + 128 * part
                if first < NLON:
                    out_ref[row, :, pl.ds(first, 128)] = jnp.where(
                        column + first < longitudes, c - s, jnp.float32(0.0)
                    )

    def loop(count, act):
        def step(i, carry):
            act(i)
            return carry

        lax.fori_loop(0, count, step, 0)

    legendre_step(0)
    pl.semaphore_wait(barrier, LEVS + PER_PLANE + PLANES - 3)
    first_move(0)
    for slot in range(1, SLOTS):
        legendre_step(slot)
        first_move(slot)
    spread_waves()
    for row in range(LOCAL_ROWS):
        cos_sum[row] = jnp.zeros((STACKED, HALF), jnp.float32)
        sin_sum[row] = jnp.zeros((STACKED, HALF), jnp.float32)
    second_move(0)
    second_move(2)
    loop(SLOTS, lambda slot: table_step(0, slot))
    second_move(1)
    second_move(4)
    last_move(0)
    last_move(2)
    second_move(3)
    last_move(4)
    last_move(1)
    loop(SLOTS, lambda slot: table_step(1, slot))
    last_move(3)

    def slot_step(slot):
        arrived(2, slot)
        loop(LOCAL_ROWS, lambda row: add_step(slot, row))

    def last_step(row):
        add_step(SLOTS - 1, row)
        finish(row)

    loop(SLOTS - 1, slot_step)
    arrived(2, SLOTS - 1)
    loop(LOCAL_ROWS, last_step)
    for stage in range(3):
        region = final.at[:, pl.ds(0, 24 if stage == 1 else 28)]
        pltpu.make_async_copy(region, region, send_sem.at[stage]).wait()


def transform(wave_table, row_longitudes, legendre_values, spectra):
    hbm = pl.BlockSpec(memory_space=pltpu.HBM)
    smem = pl.BlockSpec(memory_space=pltpu.SMEM)
    tables = pltpu.VMEM((SLOTS, LOCAL_ROWS, 3 * HALF, HALF), jnp.bfloat16)
    turns = pltpu.VMEM((SLOTS, LOCAL_ROWS, 16, HALF), jnp.float32)
    sums = pltpu.VMEM((LOCAL_ROWS, STACKED, HALF), jnp.float32)
    z_then_x = pltpu.VMEM((2, PLANES, PER_PLANE, LEVS * LOCAL_ROWS, CHANNELS), jnp.float32)
    return pl.pallas_call(
        transform_kernel,
        out_shape=jax.ShapeDtypeStruct((LOCAL_ROWS, FIELDS, NLON), jnp.float32),
        in_specs=[smem, smem, pl.BlockSpec(memory_space=pltpu.VMEM), hbm, hbm],
        out_specs=pl.BlockSpec(memory_space=pltpu.VMEM),
        scratch_shapes=[
            pltpu.VMEM((SLOTS, ROWS, DEGREES), jnp.bfloat16),
            pltpu.VMEM((SLOTS, DEGREES, CHANNELS), jnp.bfloat16),
            pltpu.VMEM((SLOTS, WAVES, LEVS * LOCAL_ROWS, CHANNELS), jnp.float32),
            pltpu.VMEM((3, WAVES, LOCAL_ROWS, LEVS, CHANNELS), jnp.float32),
            pltpu.VMEM((3, PLANES, PER_PLANE, LOCAL_ROWS, LEVS, CHANNELS), jnp.float32),
            z_then_x,
            z_then_x,
            pltpu.VMEM((SLOTS, WAVES, LOCAL_ROWS, LEVS, CHANNELS), jnp.float32),
            pltpu.VMEM((SLOTS * DEVICES, 128), jnp.float32),
            tables,
            tables,
            turns,
            turns,
            pltpu.VMEM((2, CHANNELS, 128), jnp.float32),
            sums,
            sums,
            pltpu.SemaphoreType.DMA((2, SLOTS)),
            pltpu.SemaphoreType.DMA((3,)),
            pltpu.SemaphoreType.DMA((3, SLOTS)),
            pltpu.SemaphoreType.DMA((3, SLOTS)),
        ],
        compiler_params=pltpu.CompilerParams(
            collective_id=0, has_side_effects=True, vmem_limit_bytes=48 << 20
        ),
    )(
        *(
            pltpu.with_memory_space_constraint(operand, pltpu.HBM)
            for operand in (
                wave_table,
                row_longitudes,
                wave_table.reshape(SLOTS * DEVICES // 128, 128),
                legendre_values,
                spectra,
            )
        )
    )


def per_device(legendre_values, spectra, wave_table, row_longitudes):
    return transform(wave_table, row_longitudes, legendre_values, spectra)


def solution(mesh):
    in_specs = (
        P(("wave", "lev"), None, None),
        P(("wave", "lev"), None, None),
        P(),
        P(("wave", "lev")),
    )
    out_specs = P(("wave", "lev"), None, None)
    return jax.shard_map(
        per_device, mesh=mesh, in_specs=in_specs, out_specs=out_specs, check_vma=False
    )
```

```python
import jax
import jax.numpy as jnp
from jax import lax
from jax.experimental import pallas as pl
from jax.experimental.pallas import tpu as pltpu
from jax.sharding import PartitionSpec as P

MESH = pl.DeviceIdType.MESH

SLOTS = 5
DEGREES = 1280
ROWS = 512
CHANNELS = 128
FIELDS = 64
LOCAL_ROWS = 2
PLANES = 8
PER_PLANE = 4
WAVES = PLANES * PER_PLANE
LEVS = 8
DEVICES = WAVES * LEVS
NLON = 5376
HALF = 256
SPAN = 2 * HALF
BLOCKS = 11
STACKED = BLOCKS * FIELDS

COS_TERMS = (
    0.9999999996168156,
    -19.73920863354667,
    64.93938183835107,
    -85.4564814603686,
    60.24009011425828,
    -26.392650988301078,
    7.765225095262238,
    -1.4134373617596543,
)
SIN_TERMS = (
    6.283185293777215,
    -41.341697721207424,
    81.605000209223,
    -76.70070302960839,
    42.00769493017941,
    -14.834123486306066,
    3.1498534224128543,
)


def horner(terms, square):
    total = jnp.full_like(square, terms[-1])
    for term in terms[-2::-1]:
        total = total * square + jnp.float32(term)
    return total


def cos_sin_of_turns(product, period, inverse):
    whole = jnp.round(product * inverse)
    turn = (product - whole * period) * inverse
    square = turn * turn
    return horner(COS_TERMS, square), turn * horner(SIN_TERMS, square)


def split(values):
    high = values.astype(jnp.bfloat16)
    low = (values - high.astype(jnp.float32)).astype(jnp.bfloat16)
    return high, low


def transform_kernel(
    slot_waves_ref, longitudes_ref, waves_ref, legendre_ref, spectra_ref, out_ref,
    legendre, spectra, fourier, lev_first, x_second, z_first, x_after, final,
    columns, cos_tables, sin_tables, cos_turns, sin_turns, turned, cos_sum, sin_sum,
    load_sem, send_sem, recv_sem, own_sem,
):
    wave = lax.axis_index("wave")
    lev = lax.axis_index("lev")
    z, x = lax.div(wave, PER_PLANE), lax.rem(wave, PER_PLANE)
    me = wave * LEVS + lev
    lev_peers = [lax.rem(lev + k, LEVS) for k in range(1, LEVS)]
    x_peers = [lax.rem(x + k, PER_PLANE) for k in range(1, PER_PLANE)]
    z_peers = [lax.rem(z + k, PLANES) for k in (4, 3, 5, 2, 6, 1, 7)]

    def at_lev(peer):
        return wave, peer

    def at_x(peer):
        return z * PER_PLANE + peer, lev

    def at_z(peer):
        return peer * PER_PLANE + x, lev

    def load(slot):
        return (
            pltpu.make_async_copy(spectra_ref.at[slot], spectra.at[slot], load_sem.at[0, slot]),
            pltpu.make_async_copy(legendre_ref.at[slot], legendre.at[slot], load_sem.at[1, slot]),
        )

    for slot in range(SLOTS):
        for copy in load(slot):
            copy.start()

    barrier = pltpu.get_barrier_semaphore()
    for peers, at in ((z_peers, at_z), (x_peers, at_x), (lev_peers, at_lev)):
        for peer in peers:
            pl.semaphore_signal(barrier, inc=1, device_id=at(peer), device_id_type=MESH)

    degree = lax.broadcasted_iota(jnp.int32, (DEGREES, CHANNELS), 0)

    def legendre_step(slot):
        for copy in load(slot):
            copy.wait()
        wavenumber = slot_waves_ref[me * SLOTS + slot]
        values = spectra[slot].astype(jnp.float32)
        kept = jnp.where(degree >= wavenumber, values, jnp.float32(0.0)).astype(jnp.bfloat16)
        sums = jnp.dot(legendre[slot], kept, preferred_element_type=jnp.float32)
        fourier[slot] = sums.reshape(WAVES, LEVS * LOCAL_ROWS, CHANNELS)

    def move(stage, slot, source, target, peers, own, at):
        for peer in peers:
            pltpu.make_async_remote_copy(
                src_ref=source(peer),
                dst_ref=target,
                send_sem=send_sem.at[stage],
                recv_sem=recv_sem.at[stage, slot],
                device_id=at(peer),
                device_id_type=MESH,
            ).start()
        pltpu.make_async_copy(source(own), target, own_sem.at[stage, slot]).start()

    def arrived(stage, slot):
        count = 24 if stage == 1 else 28
        region = final.at[slot, pl.ds(0, count)]
        pltpu.make_async_copy(region, region, recv_sem.at[stage, slot]).wait()
        region = final.at[slot, pl.ds(0, WAVES - count)]
        pltpu.make_async_copy(region, region, own_sem.at[stage, slot]).wait()

    def pair(peer):
        return pl.ds(peer * LOCAL_ROWS, LOCAL_ROWS)

    def plane(peer):
        return pl.ds(peer * PER_PLANE, PER_PLANE)

    def first_move(slot):
        if slot % 2:
            move(
                0, slot, lambda peer: fourier.at[slot, plane(peer)],
                z_first.at[slot // 2, z], z_peers, z, at_z,
            )
        else:
            move(
                0, slot, lambda peer: fourier.at[slot, :, pair(peer), :],
                lev_first.at[slot // 2, :, :, lev, :], lev_peers, lev, at_lev,
            )

    def second_move(slot):
        arrived(0, slot)
        if slot % 2:
            move(
                1, slot, lambda peer: z_first.at[slot // 2, :, peer],
                x_after.at[slot // 2, :, x], x_peers, x, at_x,
            )
        else:
            move(
                1, slot,
                lambda peer: lev_first.at[slot // 2].reshape(
                    PLANES, PER_PLANE, LOCAL_ROWS, LEVS, CHANNELS
                ).at[:, peer],
                x_second.at[slot // 2, :, x], x_peers, x, at_x,
            )

    def last_move(slot):
        arrived(1, slot)
        if slot % 2:
            move(
                2, slot,
                lambda peer: x_after.at[slot // 2].reshape(
                    WAVES, LEVS * LOCAL_ROWS, CHANNELS
                ).at[:, pair(peer), :],
                final.at[slot, :, :, lev, :], lev_peers, lev, at_lev,
            )
        else:
            move(
                2, slot, lambda peer: x_second.at[slot // 2, peer],
                final.at[slot, plane(z)], z_peers, z, at_z,
            )

    odd = (2 * lax.broadcasted_iota(jnp.int32, (HALF, HALF), 1) + 1).astype(jnp.float32)
    centre = (
        2 * SPAN * lax.broadcasted_iota(jnp.int32, (16, HALF), 0) + (SPAN - 1)
    ).astype(jnp.float32)

    def spread_waves():
        for part in range(SLOTS * DEVICES // 128):
            row = waves_ref[pl.ds(part, 1), :].astype(jnp.float32)
            columns[pl.ds(part * 128, 128), :] = jnp.broadcast_to(row, (128, 128)).T

    def table_step(row, slot):
        longitudes = longitudes_ref[row]
        period = (2 * longitudes).astype(jnp.float32)
        inverse = (jnp.float32(1.0) / jnp.full((8, 128), period, jnp.float32))[:1, :1]
        largest = lax.div(longitudes - 1, 2).astype(jnp.float32)
        wave_column = columns[pl.ds(slot, DEVICES, stride=SLOTS), :]
        wave_row = jnp.concatenate([wave_column[:128, :].T, wave_column[128:, :].T], axis=1)[:16, :]
        product = jnp.concatenate([wave_column, wave_column], axis=1) * odd
        table_cos, table_sin = cos_sin_of_turns(product, period, inverse)
        for table, tables in ((table_cos, cos_tables), (table_sin, sin_tables)):
            high, low = split(table)
            tables[slot, row, pl.ds(0, HALF), :] = high
            tables[slot, row, pl.ds(HALF, HALF), :] = high
            tables[slot, row, pl.ds(2 * HALF, HALF), :] = low
        weight = jnp.where(
            wave_row > largest,
            jnp.float32(0.0),
            jnp.where(wave_row == 0, jnp.float32(1.0), jnp.float32(2.0)),
        )
        block_cos, block_sin = cos_sin_of_turns(wave_row * centre, period, inverse)
        cos_turns[slot, row] = block_cos * weight
        sin_turns[slot, row] = block_sin * weight

    def add_step(slot, row):
        values = final[slot, :, row].reshape(DEVICES, CHANNELS)
        for half in range(2):
            turned[half] = values[half * 128 : half * 128 + 128, :].T
        real, imag = (
            jnp.concatenate(
                [turned[half, pl.ds(part, FIELDS, stride=2), :] for half in range(2)], axis=1
            )
            for part in range(2)
        )
        block_cos = cos_turns[slot, row]
        block_sin = sin_turns[slot, row]
        real_parts = []
        imag_parts = []
        for k in range(BLOCKS):
            c = block_cos[k : k + 1, :]
            s = block_sin[k : k + 1, :]
            high, low = split(real * c - imag * s)
            real_parts.append(jnp.concatenate([high, low, high], axis=1))
            high, low = split(real * s + imag * c)
            imag_parts.append(jnp.concatenate([high, low, high], axis=1))
        real_side = jnp.concatenate(real_parts, axis=0)
        imag_side = jnp.concatenate(imag_parts, axis=0)
        cos_sum[row] += jnp.dot(
            real_side, cos_tables[slot, row], preferred_element_type=jnp.float32
        )
        sin_sum[row] += jnp.dot(
            imag_side, sin_tables[slot, row], preferred_element_type=jnp.float32
        )

    backwards = 127 - lax.broadcasted_iota(jnp.int32, (FIELDS, 128), 1)
    column = lax.broadcasted_iota(jnp.int32, (FIELDS, 128), 1)

    def finish(row):
        longitudes = longitudes_ref[row]
        for k in range(BLOCKS):
            rows = pl.ds(k * FIELDS, FIELDS)
            for part in range(2):
                lanes = pl.ds(part * 128, 128)
                c = cos_sum[row, rows, lanes]
                s = sin_sum[row, rows, lanes]
                first = k * SPAN + 128 * (1 - part)
                values = jnp.take_along_axis(c + s, backwards, axis=1)
                out_ref[row, :, pl.ds(first, 128)] = jnp.where(
                    column + first < longitudes, values, jnp.float32(0.0)
                )
                first = k * SPAN + HALF + 128 * part
                if first < NLON:
                    out_ref[row, :, pl.ds(first, 128)] = jnp.where(
                        column + first < longitudes, c - s, jnp.float32(0.0)
                    )

    def loop(count, act):
        def step(i, carry):
            act(i)
            return carry

        lax.fori_loop(0, count, step, 0)

    legendre_step(0)
    pl.semaphore_wait(barrier, LEVS + PER_PLANE + PLANES - 3)
    first_move(0)
    for slot in range(1, SLOTS):
        legendre_step(slot)
        first_move(slot)
    spread_waves()
    for row in range(LOCAL_ROWS):
        cos_sum[row] = jnp.zeros((STACKED, HALF), jnp.float32)
        sin_sum[row] = jnp.zeros((STACKED, HALF), jnp.float32)
    second_move(0)
    second_move(2)
    loop(SLOTS, lambda slot: table_step(0, slot))
    second_move(1)
    second_move(4)
    last_move(0)
    last_move(2)
    second_move(3)
    last_move(4)
    last_move(1)
    loop(SLOTS, lambda slot: table_step(1, slot))
    last_move(3)

    def slot_step(slot):
        arrived(2, slot)
        loop(LOCAL_ROWS, lambda row: add_step(slot, row))

    def last_step(row):
        add_step(SLOTS - 1, row)
        finish(row)

    loop(SLOTS - 1, slot_step)
    arrived(2, SLOTS - 1)
    for row in range(LOCAL_ROWS):
        last_step(row)
    for stage in range(3):
        region = final.at[:, pl.ds(0, 24 if stage == 1 else 28)]
        pltpu.make_async_copy(region, region, send_sem.at[stage]).wait()


def transform(wave_table, row_longitudes, legendre_values, spectra):
    hbm = pl.BlockSpec(memory_space=pltpu.HBM)
    smem = pl.BlockSpec(memory_space=pltpu.SMEM)
    tables = pltpu.VMEM((SLOTS, LOCAL_ROWS, 3 * HALF, HALF), jnp.bfloat16)
    turns = pltpu.VMEM((SLOTS, LOCAL_ROWS, 16, HALF), jnp.float32)
    sums = pltpu.VMEM((LOCAL_ROWS, STACKED, HALF), jnp.float32)
    z_then_x = pltpu.VMEM((2, PLANES, PER_PLANE, LEVS * LOCAL_ROWS, CHANNELS), jnp.float32)
    return pl.pallas_call(
        transform_kernel,
        out_shape=jax.ShapeDtypeStruct((LOCAL_ROWS, FIELDS, NLON), jnp.float32),
        in_specs=[smem, smem, pl.BlockSpec(memory_space=pltpu.VMEM), hbm, hbm],
        out_specs=pl.BlockSpec(memory_space=pltpu.VMEM),
        scratch_shapes=[
            pltpu.VMEM((SLOTS, ROWS, DEGREES), jnp.bfloat16),
            pltpu.VMEM((SLOTS, DEGREES, CHANNELS), jnp.bfloat16),
            pltpu.VMEM((SLOTS, WAVES, LEVS * LOCAL_ROWS, CHANNELS), jnp.float32),
            pltpu.VMEM((3, WAVES, LOCAL_ROWS, LEVS, CHANNELS), jnp.float32),
            pltpu.VMEM((3, PLANES, PER_PLANE, LOCAL_ROWS, LEVS, CHANNELS), jnp.float32),
            z_then_x,
            z_then_x,
            pltpu.VMEM((SLOTS, WAVES, LOCAL_ROWS, LEVS, CHANNELS), jnp.float32),
            pltpu.VMEM((SLOTS * DEVICES, 128), jnp.float32),
            tables,
            tables,
            turns,
            turns,
            pltpu.VMEM((2, CHANNELS, 128), jnp.float32),
            sums,
            sums,
            pltpu.SemaphoreType.DMA((2, SLOTS)),
            pltpu.SemaphoreType.DMA((3,)),
            pltpu.SemaphoreType.DMA((3, SLOTS)),
            pltpu.SemaphoreType.DMA((3, SLOTS)),
        ],
        compiler_params=pltpu.CompilerParams(
            collective_id=0, has_side_effects=True, vmem_limit_bytes=48 << 20
        ),
    )(
        *(
            pltpu.with_memory_space_constraint(operand, pltpu.HBM)
            for operand in (
                wave_table,
                row_longitudes,
                wave_table.reshape(SLOTS * DEVICES // 128, 128),
                legendre_values,
                spectra,
            )
        )
    )


def per_device(legendre_values, spectra, wave_table, row_longitudes):
    return transform(wave_table, row_longitudes, legendre_values, spectra)


def solution(mesh):
    in_specs = (
        P(("wave", "lev"), None, None),
        P(("wave", "lev"), None, None),
        P(),
        P(("wave", "lev")),
    )
    out_specs = P(("wave", "lev"), None, None)
    return jax.shard_map(
        per_device, mesh=mesh, in_specs=in_specs, out_specs=out_specs, check_vma=False
    )
```
